256 devices in a mesh: gz: 4 (over z_lo, core), xy: 64 (over y, x, z_hi).
Axes of the slice: x: 4, y: 4, z: 8 (z_hi: 4, z_lo: 2; z = z_hi * 2 + z_lo), core: 2. Of those that a mesh axis runs over, the one named last changes fastest.
Arguments:
- features: float32 [64, 128, 28, 256], P('gz', 'xy'), may hold values from -6 to 6
- block_mask: int32 [32, 64, 14], P('gz', 'xy'), may hold values 0 or 1
- near_kernel_weight: float32 [27, 256, 256], P(None, None, 'xy'), may hold values from -0.078125 to 0.078125
- far_kernel_weight: float32 [27, 256, 256], P(None, None, 'xy'), may hold values from -0.078125 to 0.078125
Outputs:
- section_out: float32 [64, 128, 28, 256], P('gz', 'xy')
The draws below stay inside these ranges and needn't reach their ends.
All inputs are finite; a program needn't handle non-finite values. No bound on the sum of `block_mask` on one device may be relied on, other than what follows from the above.
Results may differ from the reference program's by a relative error of at most 0.00005.
Values sent between devices are 32-bit elements; how exact they have to be, the bound alone decides.
No kernel may reach another device: no remote copies, remote signals or barrier semaphores. Data moves between devices by JAX's collectives and lax.ppermute only.
A program may use at most 128 MiB of HBM per device.

```python
import jax
import jax.numpy as jnp
from jax import lax

C = 256
B = 2
NEAR_DILATION = 16
FAR_DILATION = 32
NY = 28
NZ = 64
NX = 128


def set_ends(values, own_key, least, top_value):
    longest = values.shape.index(max(values.shape))
    spots = []
    for shift in (0, 1):
        where = [jax.random.randint(jax.random.fold_in(own_key, axis), (), 0, length) for axis, length in enumerate(values.shape)]
        where[longest] = (where[longest] + shift) % values.shape[longest]
        spots.append(tuple(where))
    return values.at[spots[0]].set(least).at[spots[1]].set(top_value)


def shard_levels(stream_key, extent, split, least, top_value):
    def one(dim, blocks):
        heights = jax.random.uniform(jax.random.fold_in(jax.random.fold_in(stream_key, 6), dim), (blocks,), jnp.float32, least / len(split), top_value / len(split))
        return jnp.repeat(jnp.exp(heights), extent[dim] // blocks).reshape((-1,) + (1,) * (len(extent) - dim - 1))

    loudness = one(*split[0])
    for cut in split[1:]:
        loudness = loudness * one(*cut)
    return loudness


def noise(rng, extent, width, most, cuts=(), dtype=jnp.bfloat16):
    entries = width * jax.random.normal(rng, extent, jnp.float32)
    if cuts:
        entries = entries * shard_levels(rng, extent, cuts, -0.22, 0.18)
    return jnp.clip(entries, -most, most).astype(dtype)


def setup_inputs(seed: int = 0) -> dict:
    keys = jax.random.split(jax.random.key(seed), 5)
    return {
        "features": noise(keys[0], (NZ, NX, NY, C), 1.0, 6.0, ((0, 4), (1, 64)), jnp.float32),
        "block_mask": set_ends((jax.random.randint(keys[1], (NZ // B, NX // B, NY // B), 0, 5) < 3).astype(jnp.int32), jax.random.fold_in(keys[1], 1), 0, 1),
        "near_kernel_weight": noise(keys[2], (27, C, C), (27 * C) ** -0.5, 0.078125, ((2, 64),), jnp.float32),
        "far_kernel_weight": noise(keys[3], (27, C, C), (27 * C) ** -0.5, 0.078125, ((2, 64),), jnp.float32),
    }


def dilated_result(field, weight, dilation):
    channels = weight.shape[1]
    kernel = weight.reshape(3, 3, 3, channels, weight.shape[2])
    result = lax.conv_general_dilated(
        field[None], kernel, (1, 1, 1), [(dilation, dilation)] * 3,
        rhs_dilation=(dilation, dilation, dilation),
        dimension_numbers=("NDHWC", "DHWIO", "NDHWC"),
        precision=lax.Precision.HIGHEST)
    return result[0]


def reference(features, block_mask, near_kernel_weight, far_kernel_weight):
    active_blocks = jnp.repeat(jnp.repeat(jnp.repeat(block_mask, B, 0), B, 1), B, 2)
    active_blocks = active_blocks.astype(jnp.float32)[..., None]
    masked_input = active_blocks * features
    hidden_state = active_blocks * jnp.maximum(dilated_result(masked_input, near_kernel_weight, NEAR_DILATION), 0.0)
    return active_blocks * (masked_input + dilated_result(hidden_state, far_kernel_weight, FAR_DILATION))
```

```python
import jax
import jax.numpy as jnp
from jax import lax
from jax.experimental import pallas as pl
from jax.experimental.pallas import tpu as pltpu
from jax.sharding import Mesh, PartitionSpec as P

B = 2
F32, BF16 = jnp.float32, jnp.bfloat16
AXES = ("zl", "core", "y", "xh", "xl", "zh")
GROUP = ("zl", "core", "y", "xh")
X = ("xh", "xl")
NEAR = 9 * 16
FAR = 10 * 16


def split(value):
    high = value.astype(BF16)
    return high, (value - high.astype(F32)).astype(BF16)


def triple(value):
    high, low = split(value)
    return jnp.concatenate([high, low, high], 1)


def tap_matrix(buf, group, slot):
    tiles = buf[group, :, :, :, slot].reshape(32, 2, 8, 128)
    even, odd = tiles[:, 0], tiles[:, 1]
    top = lax.broadcasted_iota(jnp.int32, (32, 8, 128), 1) < 4
    left = jnp.where(top, even, pltpu.roll(odd, 4, 1)).reshape(256, 128)
    right = jnp.where(top, pltpu.roll(even, 4, 1), odd).reshape(256, 128)
    left_high, left_low = split(left)
    right_high, right_low = split(right)
    return jnp.concatenate([left_high, right_high, left_high, right_high, left_low, right_low], 1)


def dot(a, b):
    return lax.dot_general(a, b, (((1,), (1,)), ((), ())), preferred_element_type=F32)


def conv_body(spot, x_ref, *refs):
    pieces, (o_ref, buf, xn, xf, acc, mask, sem) = refs[:16], refs[16:]
    copies = []
    for n, piece in enumerate(pieces):
        group, place = spot[n, 0], spot[n, 1]
        target = buf.at[group, :, place] if n % 8 < 4 else buf.at[group, place]
        copies.append(pltpu.make_async_copy(piece, target, sem.at[n]))
        copies[-1].start()

    blank = jnp.zeros((32, 768), BF16)
    for h in range(2):
        for g in range(4):
            xn[h, g * NEAR : g * NEAR + 16] = blank[:16]
            xf[h, g * FAR : g * FAR + 32] = blank
        xn[h, 4 * NEAR :] = blank
        xf[h, 4 * FAR : 4 * FAR + 32] = blank
        xf[h, 4 * FAR + 32 :] = blank

    row = lax.broadcasted_iota(jnp.int32, (32, 256), 0)
    lane = lax.broadcasted_iota(jnp.int32, (32, 256), 1)

    @pl.loop(0, 4)
    def _(g):
        for k in range(8):
            cell = x_ref[g * 8 + k]
            active = jnp.sum(jnp.where(row == lane, cell[28:29], 0.0), 1, keepdims=True)
            active = jnp.broadcast_to(active, (32, 128))
            start = pl.multiple_of(g * NEAR + k * 16, 16)
            mask[0, pl.ds(start, 16)] = active[:16]
            mask[1, pl.ds(start, 16)] = active[16:]
            cell = jnp.where(row < 28, cell, 0.0)
            xn[0, pl.ds(start + 16, 16)] = triple(cell[:16])
            xn[1, pl.ds(start + 16, 16)] = triple(cell[16:])

    acc[...] = jnp.zeros_like(acc)
    for copy in copies:
        copy.wait()

    def add(source, plane, step, shift, margin, h_in, h_out, weight):
        count = (4 - abs(step)) * plane
        first = pl.multiple_of(max(step, 0) * plane + margin + shift, 16)
        start = max(-step, 0) * plane
        acc[h_out, start : start + count] += dot(source[h_in, pl.ds(first, count)], weight)

    for a in range(3):

        @pl.loop(0, 3)
        def _(b):
            shift = (b - 1) * 16
            weight = tap_matrix(buf, a, b * 3 + 1)
            add(xn, NEAR, a - 1, shift, 16, 0, 0, weight)
            add(xn, NEAR, a - 1, shift, 16, 1, 1, weight)
            add(xn, NEAR, a - 1, shift, 16, 0, 1, tap_matrix(buf, a, b * 3))
            add(xn, NEAR, a - 1, shift, 16, 1, 0, tap_matrix(buf, a, b * 3 + 2))

    @pl.loop(0, 4)
    def _(g):
        for h in range(2):
            for k in range(8):
                start = pl.multiple_of(g * NEAR + k * 16, 16)
                active = mask[h, pl.ds(start, 16)]
                active = jnp.concatenate([active, active], 1)
                hidden = active * jnp.maximum(acc[h, pl.ds(start, 16)], 0.0)
                start = pl.multiple_of(g * FAR + k * 16 + 32, 16)
                xf[h, pl.ds(start, 16)] = triple(hidden)

    acc[...] = jnp.zeros_like(acc)
    for a in range(3):

        @pl.loop(0, 3)
        def _(b):
            weight = tap_matrix(buf, 3, a * 3 + b)
            for h in range(2):
                add(xf, FAR, 2 * (a - 1), (b - 1) * 32, 32, h, h, weight)

    for g in range(4):
        for k in range(8):
            start = g * FAR + k * 16
            o_ref[g * 8 + k, :16] = acc[0, start : start + 16]
            o_ref[g * 8 + k, 16:] = acc[1, start : start + 16]


def convolve(spots, received, pieces):
    return pl.pallas_call(
        conv_body,
        out_shape=jax.ShapeDtypeStruct((32, 32, 256), F32),
        in_specs=[pl.BlockSpec(memory_space=pltpu.SMEM), pl.BlockSpec(memory_space=pltpu.VMEM)]
        + [pl.BlockSpec(memory_space=pl.ANY)] * 16,
        out_specs=pl.BlockSpec(memory_space=pltpu.VMEM),
        scratch_shapes=[
            pltpu.VMEM((4, 4, 4, 4, 9, 8, 128), F32),
            pltpu.VMEM((2, 4 * NEAR + 32, 768), BF16),
            pltpu.VMEM((2, 4 * FAR + 64, 768), BF16),
            pltpu.VMEM((2, 4 * FAR, 256), F32),
            pltpu.VMEM((2, 4 * NEAR, 128), F32),
            pltpu.SemaphoreType.DMA((16,)),
        ],
        compiler_params=pltpu.CompilerParams(vmem_limit_bytes=40 << 20),
        cost_estimate=pl.CostEstimate(flops=8_000_000_000, bytes_accessed=12_000_000, transcendentals=0),
    )(spots, received, *pieces)


def send(value, axis, pairs):
    return lax.ppermute(value, axis, pairs)


def shifted(value, axis):
    return [value] + [send(value, axis, [(i, (i + d) % 4) for i in range(4)]) for d in (1, 2, 3)]


def in_order(parts, which):
    return jnp.stack([lax.select_n(which[j], *parts) for j in range(4)], 0)


def tiles(weight):
    taps = weight.shape[0]
    return weight.transpose(0, 2, 1).reshape(taps, 4, 2, 128).transpose(0, 2, 1, 3).reshape(taps, 8, 128)


def along_z(mine):
    zl, zh = lax.axis_index("zl"), lax.axis_index("zh")

    def route(distance):
        return [(z, (z + (distance if z % 2 == 0 else -distance)) % 8) for z in range(8)]

    def pairs(distance):
        return [((s % 2) * 4 + s // 2, (t % 2) * 4 + t // 2) for s, t in route(distance)]

    near = send(mine, ("zl", "zh"), pairs(-1))
    next_ = send(mine, ("zl", "zh"), pairs(-2))
    far = send(mine, ("zl", "zh"), pairs(-3))
    which = []
    for j in range(4):
        ahead = (j - zh) % 4
        which.append(jnp.where(ahead == 0, 0, jnp.where(ahead == 2, 3, jnp.where((ahead == 1) == (zl == 1), 1, 2))))
    return in_order([mine, near, next_, far], which)


def gather(near_weight, far_weight):
    core, y = lax.axis_index("core"), lax.axis_index("y")
    x = lax.axis_index(X)
    every = jnp.concatenate([tiles(near_weight), tiles(far_weight[1::3])], 0).reshape(2, 2, 9, 8, 128)
    mine = jnp.where(core == 0, every[0], every[1])
    plane = along_z(mine)

    def ring(value, axis, me):
        return in_order(shifted(value, axis), [(me - j) % 4 for j in range(4)])

    rows = ring(plane[:, 0], "y", y)
    cols = ring(plane[:, 1], X, x)
    return rows, cols, core, x, y


def local(features, block_mask, near_weight, far_weight):
    active = jnp.repeat(jnp.repeat(jnp.repeat(block_mask, B, 0), B, 1), B, 2).astype(F32)
    masked = active[..., None] * features
    flags = jnp.pad(active.reshape(32, 1, 28), ((0, 0), (0, 3), (0, 228)))
    payload = jnp.concatenate([masked.reshape(32, 28, 256), flags], 1)

    rows, cols, core, x, y = gather(near_weight, far_weight)
    payload, rows, cols = lax.optimization_barrier((payload, rows, cols))
    parts = shifted(rows, X) + shifted(cols, "y")
    other = [send(part, "core", [(0, 1), (1, 0)]) for part in parts]
    received = lax.all_to_all(payload, GROUP, 0, 0, tiled=True)

    spots = []
    for side in (core, 1 - core):
        spots += [jnp.stack([2 * side, (x - d) % 4]) for d in range(4)]
        spots += [jnp.stack([2 * side + 1, (y - d) % 4]) for d in range(4)]
    result = convolve(jnp.stack(spots).astype(jnp.int32), received, parts + other)
    back = lax.all_to_all(result, GROUP, 0, 0, tiled=True)
    back = back[:, :28].reshape(16, 2, 28, 256)
    return active[..., None] * (active[..., None] * features + back)


def solution(mesh):
    fine = Mesh(mesh.devices.reshape(2, 2, 4, 2, 2, 4), AXES)
    z, xy = ("zl", "core"), ("y", "xh", "xl", "zh")
    in_specs = (P(z, xy, None, None), P(z, xy, None), P(None, None, xy), P(None, None, xy))
    return jax.shard_map(local, mesh=fine, in_specs=in_specs, out_specs=P(z, xy, None, None), check_vma=False)
```

```python
import jax
import jax.numpy as jnp
from jax import lax
from jax.experimental import pallas as pl
from jax.experimental.pallas import tpu as pltpu
from jax.sharding import Mesh, PartitionSpec as P


B = 2
F32, BF16 = jnp.float32, jnp.bfloat16
AXES = ("zl", "core", "y", "xh", "xl", "zh")
GROUP = ("zl", "core", "y", "xh")
PLANE = 28 * 8
EARLY = 14
HALVES = [(d, start) for d in (0, 1, 3, 2) for start in (0, 2)]
WHOLES = [(0, 0), (1, 0), (3, 0), (2, 0)]


def split(value):
    high = value.astype(BF16)
    return high, (value - high.astype(F32)).astype(BF16)


def triple(value):
    high, low = split(value)
    return jnp.concatenate([high, low, high], 1)


def tap_matrix(buf, core, slot):
    tiles = buf[core, :, :, :, slot].reshape(32, 2, 8, 128)
    even, odd = tiles[:, 0], tiles[:, 1]
    top = lax.broadcasted_iota(jnp.int32, (32, 8, 128), 1) < 4
    left = jnp.where(top, even, pltpu.roll(odd, 4, 1)).reshape(256, 128)
    right = jnp.where(top, pltpu.roll(even, 4, 1), odd).reshape(256, 128)
    left_high, left_low = split(left)
    right_high, right_low = split(right)
    return jnp.concatenate([left_high, right_high, left_high, right_high, left_low, right_low], 1)


def fetch(spot, pieces, table, buf, sem):
    copies = []
    for n, piece in enumerate(pieces):
        core = spot[0] if n < len(table) else 1 - spot[0]
        d, start = table[n % len(table)]
        place = (jnp.where(core == 0, spot[1], spot[2]) - d) & 3
        for e in range(piece.shape[0]):
            first, second = jnp.where(core == 0, start + e, place), jnp.where(core == 0, place, start + e)
            copies.append(pltpu.make_async_copy(piece.at[e], buf.at[core, first, second], sem.at[len(copies)]))
            copies[-1].start()
    return copies


def dot(a, b):
    return lax.dot_general(a, b, (((1,), (1,)), ((), ())), preferred_element_type=F32)


def weave(value, reach):
    row = lax.broadcasted_iota(jnp.int32, value.shape, 0) & 7
    below = jnp.where(row < reach, 0.0, pltpu.roll(value, reach, 0))
    above = jnp.where(row >= 8 - reach, 0.0, pltpu.roll(value, value.shape[0] - reach, 0))
    return below, value, above


def add(acc, source, b, step, weight, taken=(0, 28), given=(0, 28)):
    planes = range(max(0, -step), min(4, 4 - step))
    if taken[1] - taken[0] == 28:
        runs = [(planes[0], len(planes))]
    else:
        runs = [(g, 1) for g in planes]
    size = (taken[1] - taken[0]) * 8
    left = [source[b, pl.ds((g + step) * PLANE + taken[0] * 8, size + (n - 1) * PLANE)] for g, n in runs]
    product = dot(left[0] if len(left) == 1 else jnp.concatenate(left, 0), weight)
    for i, (g, n) in enumerate(runs):
        start, count = g * PLANE + given[0] * 8, size + (n - 1) * PLANE
        for half in range(2):
            acc[half, start : start + count] += product[i * count : (i + 1) * count, half * 128 : half * 128 + 128]


def prepare(x_ref, xn, mask):
    lane = lax.broadcasted_iota(jnp.int32, (PLANE, 128), 1)
    row = lax.broadcasted_iota(jnp.int32, (PLANE, 128), 0) >> 3

    @pl.loop(0, 4)
    def _(g):
        cells = pl.ds(g * 8, 8)
        for y in range(0, 32, 8):
            block = jnp.swapaxes(x_ref[cells, y : y + 8], 0, 1)
            for i in range(0, min(8, 28 - y), 2):
                cell = block[i : i + 2].reshape(16, 256)
                for b, value in enumerate(weave(cell, 1)):
                    xn[b, pl.ds(pl.multiple_of(g * PLANE + (y + i) * 8, 16), 16)] = triple(value)
            if y == 24:
                flags = jnp.concatenate([block[4, :, :128]] * 28, 0)
        active = jnp.sum(jnp.where(row == lane, flags, 0.0), 1, keepdims=True)
        mask[pl.ds(pl.multiple_of(g * PLANE, 16), PLANE)] = jnp.broadcast_to(active, (PLANE, 128))


def near_body(spot, x_ref, *refs):
    pieces, (hidden, middle, buf, xn, acc, mask, sem) = refs[:16], refs[16:]
    copies = fetch(spot, pieces, HALVES, buf, sem)
    prepare(x_ref, xn, mask)
    acc[...] = jnp.zeros_like(acc)
    for copy in copies:
        copy.wait()

    def weight(tap):
        core = jnp.where(tap < EARLY, 0, 1)
        return tap_matrix(buf, core, tap - EARLY * core)

    for a in range(3):

        @pl.loop(0, 3)
        def _(b):
            tap = a * 9 + b * 3
            add(acc, xn, b, a - 1, weight(tap + 1))
            add(acc, xn, b, a - 1, weight(tap), (0, 12), (16, 28))
            add(acc, xn, b, a - 1, weight(tap + 2), (16, 28), (0, 12))

    middle[...] = tap_matrix(buf, 1, EARLY - 1)
    for half in range(2):
        hidden[half] = mask[...] * jnp.maximum(acc[half], 0.0)


def far_body(spot, hidden, middle, *refs):
    pieces, (o_ref, buf, xf, acc, sem) = refs[:8], refs[8:]
    copies = fetch(spot, pieces, WHOLES, buf, sem)

    @pl.loop(0, 56)
    def _(n):
        rows = pl.ds(pl.multiple_of(n * 16, 16), 16)
        cell = jnp.concatenate([hidden[half, rows] for half in range(2)], 1)
        for b, value in enumerate(weave(cell, 2)):
            xf[b, rows] = triple(value)

    acc[...] = jnp.zeros_like(acc)
    add(acc, xf, 1, 0, middle[...])
    for copy in copies:
        copy.wait()

    for b in (0, 2):
        add(acc, xf, b, 0, tap_matrix(buf, b // 2, 3 - b // 2 * 3))
    for b in range(3):
        for core, a in ((0, 0), (1, 2)):
            add(acc, xf, b, 2 * (a - 1), tap_matrix(buf, core, b + core))

    @pl.loop(0, 4)
    def _(g):
        for k in range(8):
            for half in range(2):
                o_ref[g * 8 + k, :28, half * 128 : half * 128 + 128] = acc[half, pl.ds(g * PLANE + k, 28, stride=8)]


def call(body, blocks, pieces, outs, scratch, flops):
    vmem = pl.BlockSpec(memory_space=pltpu.VMEM)
    taps = pieces[0].shape[2]
    return pl.pallas_call(
        body,
        out_shape=[jax.ShapeDtypeStruct(shape, dtype) for shape, dtype in outs],
        in_specs=[pl.BlockSpec(memory_space=pltpu.SMEM)]
        + [vmem] * (len(blocks) - 1)
        + [pl.BlockSpec(memory_space=pl.ANY)] * len(pieces),
        out_specs=[vmem] * len(outs),
        scratch_shapes=[pltpu.VMEM((2, 4, 4, 4, taps, 8, 128), F32)]
        + [pltpu.VMEM(shape, dtype) for shape, dtype in scratch]
        + [pltpu.SemaphoreType.DMA((32,))],
        compiler_params=pltpu.CompilerParams(vmem_limit_bytes=60 << 20),
        cost_estimate=pl.CostEstimate(flops=flops, bytes_accessed=8_000_000, transcendentals=0),
    )(*blocks, *pieces)


def send(value, axis, pairs):
    return lax.ppermute(value, axis, pairs)


def shift(value, axis, d):
    pairs = []
    for n in range(32):
        core, y, x = n // 16, n // 4 % 4, n % 4
        if (axis == "y") == (core == 0):
            y = (y + d) % 4
        else:
            x = (x + d) % 4
        pairs.append((n, core * 16 + y * 4 + x))
    return send(value, ("core", "y", "xh", "xl"), pairs)


def in_order(parts, which):
    return jnp.stack([lax.select_n(which[j], *parts) for j in range(4)], 0)


def tiles(weight):
    taps = weight.shape[0]
    return weight.transpose(0, 2, 1).reshape(taps, 4, 2, 128).transpose(0, 2, 1, 3).reshape(taps, 8, 128)


def along_z(mine):
    zl, zh = lax.axis_index("zl"), lax.axis_index("zh")

    def pairs(distance):
        route = [(z, (z + (distance if z % 2 == 0 else -distance)) % 8) for z in range(8)]
        return [((s % 2) * 4 + s // 2, (t % 2) * 4 + t // 2) for s, t in route]

    near, following, far = [send(mine, ("zl", "zh"), pairs(-d)) for d in (1, 2, 3)]
    which = []
    for j in range(4):
        ahead = (j - zh) % 4
        which.append(jnp.where(ahead == 0, 0, jnp.where(ahead == 2, 3, jnp.where((ahead == 1) == (zl == 1), 1, 2))))
    return in_order([mine, near, following, far], which)


def gather(near_weight, far_weight, payload):
    core, y = lax.axis_index("core"), lax.axis_index("y")
    x = lax.axis_index(("xh", "xl"))
    near, far = tiles(near_weight), tiles(far_weight[1::3])
    mine = jnp.where(
        core == 0, jnp.concatenate([near[:14], far[:4]], 0), jnp.concatenate([near[14:], far[4:]], 0)
    )
    plane = along_z(mine)
    spot = jnp.stack([core, x, y]).astype(jnp.int32)
    plane, spot, _ = lax.optimization_barrier((plane, spot, payload))
    parts = [plane] + [shift(plane, "y", d) for d in (1, 2, 3)]
    me = jnp.where(core == 0, y, x)
    which = [(me - j) % 4 for j in range(4)]
    whole = in_order([part[:, :EARLY] for part in parts], which)
    late = [in_order([part[:, EARLY:] for part in parts], which)]
    low, high, late[0] = lax.optimization_barrier((whole[:2], whole[2:], late[0]))
    behind, ahead = [shift(low, "x", 1)], [shift(high, "x", 3)]
    behind.append(shift(high, "x", 1))
    ahead.insert(0, shift(low, "x", 3))
    late += [shift(late[0], "x", d) for d in (1, 3, 2)]
    early = [low, high] + behind + ahead + [shift(behind[0], "x", 1), shift(ahead[1], "x", 3)]
    pieces = [early, late]
    for piece in pieces:
        count = len(piece)
        for i in range(count):
            piece.append(send(piece[i], "core", [(0, 1), (1, 0)]))
    return pieces, spot


def section(features, block_mask, near_weight, far_weight):
    active = jnp.repeat(jnp.repeat(jnp.repeat(block_mask, B, 0), B, 1), B, 2).astype(F32)
    masked = active[..., None] * features
    flags = jnp.pad(active.reshape(32, 1, 28), ((0, 0), (0, 3), (0, 228)))
    payload = jnp.concatenate([masked.reshape(32, 28, 256), flags], 1)
    (early, late), spot = gather(near_weight, far_weight, payload)
    received = lax.all_to_all(payload, GROUP, 0, 0, tiled=True)
    rows = ((3, 4 * PLANE, 768), BF16)
    acc = ((2, 4 * PLANE, 128), F32)
    hidden, middle = call(
        near_body,
        (spot, received),
        early,
        [acc, ((256, 768), BF16)],
        [rows, acc, ((4 * PLANE, 128), F32)],
        5_000_000_000,
    )
    (result,) = call(far_body, (spot, hidden, middle), late, [((32, 32, 256), F32)], [rows, acc], 2_000_000_000)
    back = lax.all_to_all(result, GROUP, 0, 0, tiled=True)
    back = back[:, :28].reshape(16, 2, 28, 256)
    return active[..., None] * (active[..., None] * features + back)


def solution(mesh):
    fine = Mesh(mesh.devices.reshape(2, 2, 4, 2, 2, 4), AXES)
    z, xy = ("zl", "core"), ("y", "xh", "xl", "zh")
    in_specs = (P(z, xy, None, None), P(z, xy, None), P(None, None, xy), P(None, None, xy))
    return jax.shard_map(section, mesh=fine, in_specs=in_specs, out_specs=P(z, xy, None, None), check_vma=False)
```

```python
import jax
import jax.numpy as jnp
from jax import lax
from jax.experimental import pallas as pl
from jax.experimental.pallas import tpu as pltpu
from jax.sharding import Mesh, PartitionSpec as P


B = 2
F32, BF16 = jnp.float32, jnp.bfloat16
AXES = ("zl", "core", "y", "xh", "xl", "zh")
GROUP = ("zl", "core", "y", "xh")
PLANE = 28 * 8
EARLY = 14
HALVES = [(d, start) for d in (0, 1, 3, 2) for start in (0, 2)]
WHOLES = [(0, 0), (1, 0), (3, 0), (2, 0)]


def split(value):
    high = value.astype(BF16)
    return high, (value - high.astype(F32)).astype(BF16)


def triple(value):
    high, low = split(value)
    return jnp.concatenate([high, low, high], 1)


def tap_matrix(buf, core, slot):
    tiles = buf[core, :, :, :, slot].reshape(32, 2, 8, 128)
    even, odd = tiles[:, 0], tiles[:, 1]
    top = lax.broadcasted_iota(jnp.int32, (32, 8, 128), 1) < 4
    left = jnp.where(top, even, pltpu.roll(odd, 4, 1)).reshape(256, 128)
    right = jnp.where(top, pltpu.roll(even, 4, 1), odd).reshape(256, 128)
    left_high, left_low = split(left)
    right_high, right_low = split(right)
    return jnp.concatenate([left_high, right_high, left_high, right_high, left_low, right_low], 1)


def fetch(spot, pieces, table, buf, sem):
    copies = []
    for n, piece in enumerate(pieces):
        core = spot[0] if n < len(table) else 1 - spot[0]
        d, start = table[n % len(table)]
        place = (jnp.where(core == 0, spot[1], spot[2]) - d) & 3
        for e in range(piece.shape[0]):
            first, second = jnp.where(core == 0, start + e, place), jnp.where(core == 0, place, start + e)
            copies.append(pltpu.make_async_copy(piece.at[e], buf.at[core, first, second], sem.at[len(copies)]))
            copies[-1].start()
    return copies


def dot(a, b):
    return lax.dot_general(a, b, (((1,), (1,)), ((), ())), preferred_element_type=F32)


def weave(value, reach):
    row = lax.broadcasted_iota(jnp.int32, value.shape, 0) & 7
    below = jnp.where(row < reach, 0.0, pltpu.roll(value, reach, 0))
    above = jnp.where(row >= 8 - reach, 0.0, pltpu.roll(value, value.shape[0] - reach, 0))
    return below, value, above


def add(acc, source, b, step, weight, taken=(0, 28), given=(0, 28)):
    planes = range(max(0, -step), min(4, 4 - step))
    if taken[1] - taken[0] == 28:
        runs = [(planes[0], len(planes))]
    else:
        runs = [(g, 1) for g in planes]
    size = (taken[1] - taken[0]) * 8
    left = [source[b, pl.ds((g + step) * PLANE + taken[0] * 8, size + (n - 1) * PLANE)] for g, n in runs]
    product = dot(left[0] if len(left) == 1 else jnp.concatenate(left, 0), weight)
    for i, (g, n) in enumerate(runs):
        start, count = g * PLANE + given[0] * 8, size + (n - 1) * PLANE
        for half in range(2):
            acc[half, start : start + count] += product[i * count : (i + 1) * count, half * 128 : half * 128 + 128]


def prepare(x_ref, xn, mask):
    lane = lax.broadcasted_iota(jnp.int32, (PLANE, 128), 1)
    row = lax.broadcasted_iota(jnp.int32, (PLANE, 128), 0) >> 3

    @pl.loop(0, 4)
    def _(g):
        cells = pl.ds(g * 8, 8)
        for y in range(0, 32, 8):
            block = jnp.swapaxes(x_ref[cells, y : y + 8], 0, 1)
            for i in range(0, min(8, 28 - y), 2):
                cell = block[i : i + 2].reshape(16, 256)
                for b, value in enumerate(weave(cell, 1)):
                    xn[b, pl.ds(pl.multiple_of(g * PLANE + (y + i) * 8, 16), 16)] = triple(value)
            if y == 24:
                flags = jnp.concatenate([block[4, :, :128]] * 28, 0)
        active = jnp.sum(jnp.where(row == lane, flags, 0.0), 1, keepdims=True)
        mask[pl.ds(pl.multiple_of(g * PLANE, 16), PLANE)] = jnp.broadcast_to(active, (PLANE, 128))


def near_body(spot, x_ref, *refs):
    pieces, (hidden, middle, buf, xn, acc, mask, sem) = refs[:16], refs[16:]
    copies = fetch(spot, pieces, HALVES, buf, sem)
    prepare(x_ref, xn, mask)
    acc[...] = jnp.zeros_like(acc)
    for copy in copies:
        copy.wait()

    def weight(tap):
        core = jnp.where(tap < EARLY, 0, 1)
        return tap_matrix(buf, core, tap - EARLY * core)

    for a in range(3):

        @pl.loop(0, 3)
        def _(b):
            tap = a * 9 + b * 3
            add(acc, xn, b, a - 1, weight(tap + 1))
            add(acc, xn, b, a - 1, weight(tap), (0, 12), (16, 28))
            add(acc, xn, b, a - 1, weight(tap + 2), (16, 28), (0, 12))

    middle[...] = tap_matrix(buf, 1, EARLY - 1)
    for half in range(2):
        hidden[half] = mask[...] * jnp.maximum(acc[half], 0.0)


def far_body(spot, hidden, middle, *refs):
    pieces, (o_ref, buf, xf, acc, sem) = refs[:8], refs[8:]
    copies = fetch(spot, pieces, WHOLES, buf, sem)

    @pl.loop(0, 56)
    def _(n):
        rows = pl.ds(pl.multiple_of(n * 16, 16), 16)
        cell = jnp.concatenate([hidden[half, rows] for half in range(2)], 1)
        for b, value in enumerate(weave(cell, 2)):
            xf[b, rows] = triple(value)

    acc[...] = jnp.zeros_like(acc)
    add(acc, xf, 1, 0, middle[...])
    for copy in copies:
        copy.wait()

    for b in (0, 2):
        add(acc, xf, b, 0, tap_matrix(buf, b // 2, 3 - b // 2 * 3))
    for b in range(3):
        for core, a in ((0, 0), (1, 2)):
            add(acc, xf, b, 2 * (a - 1), tap_matrix(buf, core, b + core))

    @pl.loop(0, 4)
    def _(g):
        for k in range(8):
            for half in range(2):
                o_ref[g * 8 + k, :28, half * 128 : half * 128 + 128] = acc[half, pl.ds(g * PLANE + k, 28, stride=8)]


def call(body, blocks, pieces, outs, scratch, flops):
    vmem = pl.BlockSpec(memory_space=pltpu.VMEM)
    taps = pieces[0].shape[2]
    return pl.pallas_call(
        body,
        out_shape=[jax.ShapeDtypeStruct(shape, dtype) for shape, dtype in outs],
        in_specs=[pl.BlockSpec(memory_space=pltpu.SMEM)]
        + [vmem] * (len(blocks) - 1)
        + [pl.BlockSpec(memory_space=pl.ANY)] * len(pieces),
        out_specs=[vmem] * len(outs),
        scratch_shapes=[pltpu.VMEM((2, 4, 4, 4, taps, 8, 128), F32)]
        + [pltpu.VMEM(shape, dtype) for shape, dtype in scratch]
        + [pltpu.SemaphoreType.DMA((32,))],
        compiler_params=pltpu.CompilerParams(vmem_limit_bytes=60 << 20),
        cost_estimate=pl.CostEstimate(flops=flops, bytes_accessed=8_000_000, transcendentals=0),
    )(*blocks, *pieces)


def send(value, axis, pairs):
    return lax.ppermute(value, axis, pairs)


def shift(value, axis, d):
    pairs = []
    for n in range(32):
        core, y, x = n // 16, n // 4 % 4, n % 4
        if (axis == "y") == (core == 0):
            y = (y + d) % 4
        else:
            x = (x + d) % 4
        pairs.append((n, core * 16 + y * 4 + x))
    return send(value, ("core", "y", "xh", "xl"), pairs)


def in_order(parts, which):
    return jnp.stack([lax.select_n(which[j], *parts) for j in range(4)], 0)


def tiles(weight):
    taps = weight.shape[0]
    return weight.transpose(0, 2, 1).reshape(taps, 4, 2, 128).transpose(0, 2, 1, 3).reshape(taps, 8, 128)


def along_z(mine):
    zl, zh = lax.axis_index("zl"), lax.axis_index("zh")

    def pairs(distance):
        route = [(z, (z + (distance if z % 2 == 0 else -distance)) % 8) for z in range(8)]
        return [((s % 2) * 4 + s // 2, (t % 2) * 4 + t // 2) for s, t in route]

    near, following, far = [send(mine, ("zl", "zh"), pairs(-d)) for d in (1, 2, 3)]
    which = []
    for j in range(4):
        ahead = (j - zh) % 4
        which.append(jnp.where(ahead == 0, 0, jnp.where(ahead == 2, 3, jnp.where((ahead == 1) == (zl == 1), 1, 2))))
    return in_order([mine, near, following, far], which)


def gather(near_weight, far_weight, payload):
    core, y = lax.axis_index("core"), lax.axis_index("y")
    x = lax.axis_index(("xh", "xl"))
    near, far = tiles(near_weight), tiles(far_weight[1::3])
    mine = jnp.where(
        core == 0, jnp.concatenate([near[:14], far[:4]], 0), jnp.concatenate([near[14:], far[4:]], 0)
    )
    plane = along_z(mine)
    spot = jnp.stack([core, x, y]).astype(jnp.int32)
    plane, spot, _ = lax.optimization_barrier((plane, spot, payload))
    parts = [plane] + [shift(plane, "y", d) for d in (1, 2, 3)]
    me = jnp.where(core == 0, y, x)
    which = [(me - j) % 4 for j in range(4)]
    whole = in_order([part[:, :EARLY] for part in parts], which)
    late = [in_order([part[:, EARLY:] for part in parts], which)]
    low, high, late[0] = lax.optimization_barrier((whole[:2], whole[2:], late[0]))
    behind, ahead = [shift(low, "x", 1)], [shift(high, "x", 3)]
    behind.append(shift(high, "x", 1))
    ahead.insert(0, shift(low, "x", 3))
    late += [shift(late[0], "x", d) for d in (1, 3)]
    late.append(shift(late[0], "x", 2))
    early = [low, high] + behind + ahead + [shift(behind[0], "x", 1), shift(ahead[1], "x", 3)]
    received = lax.all_to_all(payload, GROUP, 0, 0, tiled=True)
    received, early[0] = lax.optimization_barrier((received, early[0]))
    pieces = [early, late]
    for piece in pieces:
        count = len(piece)
        for i in range(count):
            piece.append(send(piece[i], "core", [(0, 1), (1, 0)]))
    return pieces, spot, received


def section(features, block_mask, near_weight, far_weight):
    active = jnp.repeat(jnp.repeat(jnp.repeat(block_mask, B, 0), B, 1), B, 2).astype(F32)
    masked = active[..., None] * features
    flags = jnp.pad(active.reshape(32, 1, 28), ((0, 0), (0, 3), (0, 228)))
    payload = jnp.concatenate([masked.reshape(32, 28, 256), flags], 1)
    (early, late), spot, received = gather(near_weight, far_weight, payload)
    rows = ((3, 4 * PLANE, 768), BF16)
    acc = ((2, 4 * PLANE, 128), F32)
    hidden, middle = call(
        near_body,
        (spot, received),
        early,
        [acc, ((256, 768), BF16)],
        [rows, acc, ((4 * PLANE, 128), F32)],
        5_000_000_000,
    )
    (result,) = call(far_body, (spot, hidden, middle), late, [((32, 32, 256), F32)], [rows, acc], 2_000_000_000)
    back = lax.all_to_all(result, GROUP, 0, 0, tiled=True)
    back = back[:, :28].reshape(16, 2, 28, 256)
    return active[..., None] * (active[..., None] * features + back)


def solution(mesh):
    fine = Mesh(mesh.devices.reshape(2, 2, 4, 2, 2, 4), AXES)
    z, xy = ("zl", "core"), ("y", "xh", "xl", "zh")
    in_specs = (P(z, xy, None, None), P(z, xy, None), P(None, None, xy), P(None, None, xy))
    return jax.shard_map(section, mesh=fine, in_specs=in_specs, out_specs=P(z, xy, None, None), check_vma=False)
```
